32 devices in a mesh: head: 2 (over x), seq: 16 (over z, y, core).
Axes of the slice: x: 2, y: 2, z: 4, core: 2. Of those that a mesh axis runs over, the one named last changes fastest.
Arguments:
- query_rows: bfloat16 [16, 2, 256, 256], P('seq', 'head'), may hold values from -6 to 6
- key_rows: bfloat16 [16, 2, 256, 256], P('seq', 'head'), may hold values from -6 to 6
- value_rows: bfloat16 [16, 2, 256, 256], P('seq', 'head'), may hold values from -6 to 6
- output_grad: bfloat16 [16, 2, 256, 256], P('seq', 'head'), may hold values from -384 to 384
- output_rows: bfloat16 [16, 2, 256, 256], P('seq', 'head'), may hold values from -1.5 to 1.5
- row_logsumexp: float32 [8192, 2], P('seq', 'head')
- chosen_owner: int32 [128, 2], P('seq'), may hold values from 0 to 15, all different within a row; in each aligned block of 8 rows (0 to 7, 8 to 15, ...) at most 2 rows name the same one
- chosen_cubes: int32 [128, 2, 8], P('seq'), may hold values 0 or 1
Outputs:
- query_grad: bfloat16 [16, 2, 256, 256], P('seq', 'head')
- key_grad: bfloat16 [16, 2, 256, 256], P('seq', 'head')
- value_grad: bfloat16 [16, 2, 256, 256], P('seq', 'head')
The draws below stay inside these ranges and needn't reach their ends.
Inputs may be any that keep to these rules, and one draw needn't show every extreme that they name: `chosen_owner`: each query cube names 2 different indices; the 8 query cubes held by one index of seq name any one index at most 2 times, and exactly 2 times for some index in every draw. `chosen_cubes`: 1 marks a selected key cube.
All inputs are finite; a program needn't handle non-finite values. No bound on the sum of `chosen_cubes` on one device may be relied on, other than what follows from the above.
Results may differ from the reference program's by a relative error of at most 0.0053.
Values may be sent and summed in bfloat16 or wider, within the bound.
A program may use at most 64 MiB of HBM per device.

```python
import math
import jax
import jax.numpy as jnp
import numpy as np
from jax import lax

HD = 128
CUBE = 64
CUBE_DEV = 8
CAP = 2
SEL = 2
HEADS = 2
TOK_DEV = 512
TOKENS = 8192
NQC = 128
PIECE = 256
N_HEAD = 2
N_SEQ = 16


def draw_row_logsumexp(key, part):
    centre = jnp.log(jnp.float32(SEL * CUBE_DEV * CUBE) * 0.5) + 0.5
    spread = 0.3 * jnp.clip(jax.random.normal(key, (TOKENS, HEADS), jnp.float32), -6.0, 6.0)
    return centre + spread


def touch_ends(values, rng, low, largest):
    extent = values.shape
    index_at = [jax.random.randint(jax.random.fold_in(rng, axis), (), 0, extent[axis]) for axis in range(len(extent))]
    values = values.at[tuple(index_at)].set(low)
    longest = extent.index(max(extent))
    index_at[longest] = (index_at[longest] + 1) % extent[longest]
    return values.at[tuple(index_at)].set(largest)


def steps_of(stream_key, dims, shards, least, high):
    gain = 1.0
    for position, shards_of in shards:
        steps = jax.random.uniform(jax.random.fold_in(jax.random.fold_in(stream_key, 6), position), (shards_of,), jnp.float32, least / len(shards), high / len(shards))
        gain = gain * jnp.repeat(jnp.exp(steps), dims[position] // shards_of).reshape((-1,) + (1,) * (len(dims) - 1 - position))
    return gain


def routed_block(rng, own, number, rows, amount, top, most, lean):
    sequence = jax.random.permutation(rng, amount)
    heavy_load, usual = shares(amount, rows * top, most, lean, True), shares(amount, rows * top, most, lean, False)
    places = jnp.arange(amount)

    def named(tallies, turn):
        used = int((tallies > 0).sum())
        fixed = max(1, used // 4)
        shifted = fixed + (places - fixed + turn * (used - fixed)) % max(1, amount - fixed)
        return jnp.zeros((amount,), jnp.int32).at[sequence[jnp.where(places < fixed, places, shifted)]].set(jnp.asarray(tallies, jnp.int32))

    tallies = jnp.where(number % 4 == 0, named(heavy_load, number // 4), named(usual, number - number // 4 - 1))
    mixed = jax.random.permutation(jax.random.fold_in(own, 3), amount)
    donor, sink = mixed[0:amount // 2 * 2:2], mixed[1:amount // 2 * 2:2]
    margin = jnp.minimum(tallies[donor] - 1, most - tallies[sink]) // 2
    margin = jnp.where((donor == sequence[0]) | (sink == sequence[0]) | (tallies[sink] == 0), 0, jnp.maximum(margin, 0))
    shifted = jax.random.randint(jax.random.fold_in(own, 4), (amount // 2,), 0, 1 << 20) % (margin + 1)
    tallies = tallies.at[donor].add(-shifted).at[sink].add(shifted)
    labels = jnp.searchsorted(jnp.cumsum(tallies), jnp.arange(rows * top), side="right").astype(jnp.int32)
    table = labels.reshape(top, rows).T
    table = table[jax.random.permutation(jax.random.fold_in(own, 1), rows)]
    turn = jax.random.randint(jax.random.fold_in(own, 2), (rows, 1), 0, top)
    return jnp.take_along_axis(table, (jnp.arange(top)[None, :] + turn) % top, axis=1)


def shares(count, total, limit, lean, full):
    loads = [(1 << 20) // math.isqrt(grade ** lean) + 1 for grade in range(1, count + 1)]
    largest = limit if full else min(limit, max(-(-total // count), total * loads[0] // sum(loads)))
    least = 1 if total - largest >= count - 1 else 0
    holding, spare = [largest] + [least] * (count - 1), total - largest - least * (count - 1)
    while spare > 0:
        free = [i for i in range(1, count) if holding[i] < largest] or [i for i in range(1, count) if holding[i] < limit]
        pool, left = sum([loads[i] for i in free]), spare
        for i in free:
            more = min(limit - holding[i], max(1, left * loads[i] // pool), spare)
            holding[i] = holding[i] + more
            spare = spare - more
    return np.array(holding)


def centred(own_key, extent, scale, bound, split=(), kind=jnp.bfloat16):
    entries = scale * jax.random.normal(own_key, extent, jnp.float32)
    if split:
        entries = entries * steps_of(own_key, extent, split, -0.22, 0.18)
    return jnp.clip(entries, -bound, bound).astype(kind)


def setup_inputs(seed: int = 0) -> dict:
    seeds = jax.random.split(jax.random.key(seed), 9)
    query_rows = centred(seeds[0], (N_SEQ, N_HEAD, PIECE, HEADS * HD), 1.0, 6.0, ((0, 16), (1, 2)))
    key_rows = centred(seeds[1], (N_SEQ, N_HEAD, PIECE, HEADS * HD), 1.0, 6.0, ((0, 16), (1, 2)))
    value_rows = centred(seeds[2], (N_SEQ, N_HEAD, PIECE, HEADS * HD), 1.0, 6.0, ((0, 16), (1, 2)))
    output_grad = centred(seeds[3], (N_SEQ, N_HEAD, PIECE, HEADS * HD), 64.0, 384.0, ((0, 16), (1, 2)))
    output_rows = centred(seeds[4], (N_SEQ, N_HEAD, PIECE, HEADS * HD), 0.25, 1.5, ((0, 16), (1, 2)))
    row_logsumexp = draw_row_logsumexp(jax.random.fold_in(seeds[8], 71), 0)
    chosen_owner_keys = jax.random.split(jax.random.fold_in(seeds[6], 1), NQC // CUBE_DEV)
    chosen_owner_turns = jax.random.permutation(jax.random.fold_in(seeds[6], 3), NQC // CUBE_DEV)
    chosen_owner = jax.vmap(lambda own, number: routed_block(jax.random.fold_in(seeds[6], 2), own, number, CUBE_DEV, N_SEQ, SEL, CAP, 2))(chosen_owner_keys, chosen_owner_turns).reshape((NQC, SEL))
    chosen_cubes = touch_ends((jax.random.randint(seeds[7], (NQC, SEL, CUBE_DEV), 0, 2) < 1).astype(jnp.int32), jax.random.fold_in(seeds[7], 1), 0, 1)
    return dict(query_rows=query_rows, key_rows=key_rows, value_rows=value_rows, output_grad=output_grad, output_rows=output_rows, row_logsumexp=row_logsumexp, chosen_owner=chosen_owner, chosen_cubes=chosen_cubes)


def reference(query_rows, key_rows, value_rows, output_grad, output_rows, row_logsumexp, chosen_owner, chosen_cubes):

    def to_heads(array):
        return array.reshape(TOKENS, HEADS, HD).transpose(1, 0, 2)
    softmax_scale = 1.0 / math.sqrt(HD)
    cube_group = 8
    block_count = NQC // cube_group
    owners = chosen_owner.astype(jnp.int32).reshape(block_count, cube_group, SEL)
    masks = chosen_cubes.astype(jnp.float32).reshape(block_count, cube_group, SEL, CUBE_DEV)

    def one_head(head_arrays):
        query_head, key_head, value_head, grad_head, output_head, log_head = head_arrays
        row_delta = lax.optimization_barrier(jnp.sum(grad_head.astype(jnp.float32) * output_head.astype(jnp.float32), axis=-1))
        key_blocks = key_head.reshape(N_SEQ, TOK_DEV, HD)
        value_blocks = value_head.reshape(N_SEQ, TOK_DEV, HD)

        def cube_step(totals, cube_block):
            grad_k, grad_v = totals
            owner_part, mask_part, query_part, grad_part, log_part, delta_part = cube_block
            key_sel = jnp.take(key_blocks, owner_part, axis=0).astype(jnp.float32)
            value_sel = jnp.take(value_blocks, owner_part, axis=0).astype(jnp.float32)
            query_wide = query_part.astype(jnp.float32)
            grad_wide = grad_part.astype(jnp.float32)
            scores = jnp.einsum('crd,cjkd->cjrk', query_wide, key_sel) * softmax_scale
            key_keep = jnp.repeat(mask_part, CUBE, axis=-1)
            weights = jnp.exp(scores - log_part[:, None, :, None]) * key_keep[:, :, None, :]
            dweights = jnp.einsum('crd,cjkd->cjrk', grad_wide, value_sel)
            dscores = weights * (dweights - delta_part[:, None, :, None])
            weights_low = lax.optimization_barrier(weights.astype(jnp.bfloat16)).astype(jnp.float32)
            dscores_low = lax.optimization_barrier(dscores.astype(jnp.bfloat16)).astype(jnp.float32)
            value_terms = jnp.einsum('cjrk,crd->cjkd', weights_low, grad_wide)
            key_terms = softmax_scale * jnp.einsum('cjrk,crd->cjkd', dscores_low, query_wide)
            query_terms = softmax_scale * jnp.einsum('cjrk,cjkd->crd', dscores_low, key_sel)
            flat_owner = owner_part.reshape(-1)
            grad_k = grad_k.at[flat_owner].add(key_terms.reshape(-1, TOK_DEV, HD))
            grad_v = grad_v.at[flat_owner].add(value_terms.reshape(-1, TOK_DEV, HD))
            return ((grad_k, grad_v), query_terms)
        zero_init = jnp.zeros((N_SEQ, TOK_DEV, HD), jnp.float32)
        inputs = (owners, masks, query_head.reshape(block_count, cube_group, CUBE, HD), grad_head.reshape(block_count, cube_group, CUBE, HD), log_head.reshape(block_count, cube_group, CUBE), row_delta.reshape(block_count, cube_group, CUBE))
        (grad_k, grad_v), query_terms = lax.scan(cube_step, (zero_init, zero_init), inputs)
        return (query_terms.reshape(TOKENS, HD), grad_k.reshape(TOKENS, HD), grad_v.reshape(TOKENS, HD))
    head_inputs = (to_heads(query_rows), to_heads(key_rows), to_heads(value_rows), to_heads(output_grad), to_heads(output_rows), row_logsumexp.transpose(1, 0))
    grad_q, grad_k, grad_v = lax.map(one_head, head_inputs)

    def to_rows(array):
        return array.transpose(1, 0, 2).reshape(N_SEQ, N_HEAD, PIECE, HEADS * HD).astype(jnp.bfloat16)
    return (to_rows(grad_q), to_rows(grad_k), to_rows(grad_v))
```

```python
import functools
import math

import jax
import jax.numpy as jnp
from jax import lax
from jax.experimental import pallas as pl
from jax.experimental.pallas import tpu as pltpu
from jax.sharding import PartitionSpec as P

CAP = 2
LOG2E = math.log2(math.e)
NT = (((1,), (1,)), ((), ()))
NN = (((1,), (0,)), ((), ()))


def kernel(
    heads, seqs, sel,
    owner_ref, q_ref, k_ref, v_ref, g_ref, o_ref, lm_ref,
    oq_ref, ok_ref, ov_ref,
    qh, gh, kh, vh, kt, dsend, dlt, lm, tab_f, tab_x, ret_ix,
    sqd, rqd, smeta, rmeta, dk, dv, gq, gk, gv, sret, ret,
    loc_sem, hs_sem, hr_sem, ds_sem, dr_sem, ms_sem, mr_sem, rs_sem, rr_sem, os_sem, or_sem,
):
    me_h = lax.axis_index("head")
    me_s = lax.axis_index("seq")
    cubes, rows, width = qh.shape
    piece = q_ref.shape[0]
    pairs = cubes * sel
    scale = 1.0 / math.sqrt(width)
    half = seqs // 2
    pow2 = seqs & (seqs - 1) == 0

    def goes_to(i):
        if not pow2:
            return (me_s + i) % seqs
        d = me_s
        for b in range(seqs.bit_length() - 1):
            w = 1 << b
            d = d + ((i // w) % 2) * w * (1 - 2 * ((me_s // w) % 2))
        return d

    def comes_from(i):
        return goes_to(i) if pow2 else (me_s + seqs - i) % seqs

    barrier = pltpu.get_barrier_semaphore()
    for t in range(1, heads):
        pl.semaphore_signal(barrier, inc=1, device_id={"head": (me_h + t) % heads, "seq": me_s})

    @pl.loop(1, seqs)
    def _(i):
        pl.semaphore_signal(barrier, inc=1, device_id={"head": me_h, "seq": goes_to(i)})

    def cols(h):
        return pl.ds(pl.multiple_of(h * width, width), width)

    def rows_of(h):
        return pl.ds(h * piece, piece)

    srcs = (q_ref, g_ref, k_ref, v_ref)
    dsts = (qh, gh, kh, vh)
    own = [
        pltpu.make_async_copy(s.at[:, :, cols(me_h)], d.at[rows_of(me_h)], loc_sem.at[n])
        for n, (s, d) in enumerate(zip(srcs, dsts))
    ]
    for c in own:
        c.start()

    for a in range(heads):
        for x in range(piece):
            prod = g_ref[x, :, a * width:(a + 1) * width].astype(jnp.float32) * o_ref[
                x, :, a * width:(a + 1) * width
            ].astype(jnp.float32)
            both = jnp.concatenate([prod] * CAP, axis=0)
            line = jnp.sum(both.T, axis=0, keepdims=True)
            dsend[a, x] = jnp.broadcast_to(line, (8, CAP * rows))

    lm[0:pairs] = lm_ref[...]
    lm[pairs] = jnp.full(lm.shape[1:], jnp.inf, jnp.float32)

    pl.semaphore_wait(barrier, heads - 1 + seqs - 1)

    head_copies = []
    for t in range(1, heads):
        to = (me_h + t) % heads
        for n, (s, d) in enumerate(zip(srcs, dsts)):
            head_copies.append((n, pltpu.make_async_remote_copy(
                src_ref=s.at[:, :, cols(to)], dst_ref=d.at[rows_of(me_h)],
                send_sem=hs_sem.at[t, n], recv_sem=hr_sem.at[t, n],
                device_id={"head": to, "seq": me_s})))
        head_copies.append((4, pltpu.make_async_remote_copy(
            src_ref=dsend.at[to], dst_ref=dlt.at[rows_of(me_h)],
            send_sem=hs_sem.at[t, 4], recv_sem=hr_sem.at[t, 4],
            device_id={"head": to, "seq": me_s})))
    for n in (0, 1, 4, 2, 3):
        for m, c in head_copies:
            if m == n:
                c.start()
    dlt[rows_of(me_h)] = dsend[me_h]

    @pl.loop(0, seqs)
    def _(d):
        count = jnp.int32(0)
        f = [jnp.int32(pairs)] * CAP
        xs = [jnp.int32(0)] * CAP
        for x in range(cubes):
            for j in range(sel):
                hit = owner_ref[x * sel + j] == d
                for c in range(CAP):
                    take = hit & (count == c)
                    f[c] = jnp.where(take, x * sel + j, f[c])
                    xs[c] = jnp.where(take, x, xs[c])
                count = count + hit.astype(jnp.int32)
        for c in range(CAP):
            tab_f[d * CAP + c] = f[c]
            tab_x[d * CAP + c] = xs[c]

    for c in own[:2]:
        c.wait()
    for m, c in head_copies:
        if m in (0, 1, 4):
            c.wait_recv()

    lane = lax.broadcasted_iota(jnp.int32, (8, CAP * rows), 1)

    def fill(d, slot, qd, meta):
        lines, deltas = None, None
        for c in range(CAP):
            x = tab_x[d * CAP + c]
            qd[slot, 0, c * rows:(c + 1) * rows] = qh[x]
            qd[slot, 1, c * rows:(c + 1) * rows] = gh[x]
            l_c, d_c = lm[tab_f[d * CAP + c]], dlt[x]
            lines = l_c if c == 0 else jnp.where(lane < c * rows, lines, l_c)
            deltas = d_c if c == 0 else jnp.where(lane < c * rows, deltas, d_c)
        meta[slot, 0:8] = lines
        meta[slot, 8:16] = deltas

    def data_copy(i, slot):
        dev = {"head": me_h, "seq": goes_to(i)}
        return (
            pltpu.make_async_remote_copy(
                src_ref=sqd.at[slot], dst_ref=rqd.at[slot], send_sem=ds_sem.at[slot],
                recv_sem=dr_sem.at[slot], device_id=dev),
            pltpu.make_async_remote_copy(
                src_ref=smeta.at[slot], dst_ref=rmeta.at[slot], send_sem=ms_sem.at[slot],
                recv_sem=mr_sem.at[slot], device_id=dev),
        )

    def back_copy(i, slot):
        return pltpu.make_async_remote_copy(
            src_ref=sret.at[slot], dst_ref=ret.at[pl.ds(me_s * CAP, CAP)],
            send_sem=rs_sem.at[slot], recv_sem=rr_sem.at[slot],
            device_id={"head": me_h, "seq": comes_from(i)})

    def send(i, slot):
        fill(goes_to(i), slot, sqd, smeta)
        for c in data_copy(i, slot):
            c.start()

    send(seqs - 1, 0)

    @pl.loop(1, half)
    def _(k):
        send(seqs - 1 - k, 2 * k)
        send(k, 2 * k + 1)

    fill(me_s, 1, rqd, rmeta)

    for c in own[2:]:
        c.wait()
    for m, c in head_copies:
        if m in (2, 3):
            c.wait_recv()

    keys = cubes * rows
    kt[...] = kh[...].reshape(keys, width).astype(jnp.float32).T.astype(jnp.bfloat16)
    dk[...] = jnp.zeros_like(dk)
    dv[...] = jnp.zeros_like(dv)
    wide = CAP * rows

    def work(k):
        base = 2 * k
        qb = jnp.concatenate([rqd[base, 0], rqd[base + 1, 0]], axis=0)
        gb = jnp.concatenate([rqd[base, 1], rqd[base + 1, 1]], axis=0)
        meta = jnp.concatenate([rmeta[base], rmeta[base + 1]], axis=1)
        kk = kh[...].reshape(keys, width)
        vv = vh[...].reshape(keys, width)
        st = lax.dot_general(kk, qb, NT, preferred_element_type=jnp.float32)
        dpt = lax.dot_general(vv, gb, NT, preferred_element_type=jnp.float32)
        st = st.reshape(cubes, rows, 2 * wide)
        p = jnp.exp2(st * (scale * LOG2E) - meta[0:8][:, None, :])
        ds = p * (dpt.reshape(cubes, rows, 2 * wide) - meta[8:9][:, None, :])
        pb = p.astype(jnp.bfloat16).reshape(keys, 2 * wide)
        dsb = ds.astype(jnp.bfloat16).reshape(keys, 2 * wide)
        dv[...] += lax.dot_general(pb, gb, NN, preferred_element_type=jnp.float32)
        dk[...] += lax.dot_general(dsb, qb, NN, preferred_element_type=jnp.float32)
        dqt = lax.dot_general(kt[...], dsb, NN, preferred_element_type=jnp.float32)
        dq = (dqt.T * scale).astype(jnp.bfloat16)
        return dq.reshape(2, CAP, rows, width)

    def arrive(i, slot):
        for c in data_copy(i, slot):
            c.wait_recv()

    arrive(seqs - 1, 0)
    dq = work(0)
    sret[0] = dq[0]
    back_copy(seqs - 1, 0).start()
    ret[pl.ds(me_s * CAP, CAP)] = dq[1]

    @pl.loop(1, half)
    def _(k):
        arrive(seqs - 1 - k, 2 * k)
        arrive(k, 2 * k + 1)
        dq = work(k)
        sret[2 * k] = dq[0]
        back_copy(seqs - 1 - k, 2 * k).start()
        sret[2 * k + 1] = dq[1]
        back_copy(k, 2 * k + 1).start()

    gk[...] = (dk[...] * scale).astype(jnp.bfloat16).reshape(gk.shape)
    gv[...] = dv[...].astype(jnp.bfloat16).reshape(gv.shape)
    grads, outs = (gk, gv, gq), (ok_ref, ov_ref, oq_ref)

    def out_copies(n):
        remote = []
        for t in range(1, heads):
            to = (me_h + t) % heads
            remote.append(pltpu.make_async_remote_copy(
                src_ref=grads[n].at[rows_of(to)], dst_ref=outs[n].at[:, :, cols(me_h)],
                send_sem=os_sem.at[t, n], recv_sem=or_sem.at[t, n],
                device_id={"head": to, "seq": me_s}))
        local = pltpu.make_async_copy(
            grads[n].at[rows_of(me_h)], outs[n].at[:, :, cols(me_h)], loc_sem.at[4 + n])
        return remote + [local]

    final = out_copies(0) + out_copies(1)
    for c in final:
        c.start()

    for x in range(cubes):
        for j in range(sel):
            d = owner_ref[x * sel + j]
            before = jnp.int32(0)
            for y in range(x):
                for m in range(sel):
                    before = before + (owner_ref[y * sel + m] == d).astype(jnp.int32)
            ret_ix[x * sel + j] = d * CAP + jnp.minimum(before, CAP - 1)

    back_copy(seqs - 1, 0).wait_recv()

    @pl.loop(1, half)
    def _(k):
        back_copy(seqs - 1 - k, 2 * k).wait_recv()
        back_copy(k, 2 * k + 1).wait_recv()

    for x in range(cubes):
        total = ret[ret_ix[x * sel]].astype(jnp.float32)
        for j in range(1, sel):
            total = total + ret[ret_ix[x * sel + j]].astype(jnp.float32)
        gq[x] = total.astype(jnp.bfloat16)
    last = out_copies(2)
    for c in last:
        c.start()

    for m, c in head_copies:
        c.wait_send()

    for c in data_copy(seqs - 1, 0):
        c.wait_send()
    back_copy(seqs - 1, 0).wait_send()

    @pl.loop(1, half)
    def _(k):
        for i, slot in ((seqs - 1 - k, 2 * k), (k, 2 * k + 1)):
            for c in data_copy(i, slot):
                c.wait_send()
            back_copy(i, slot).wait_send()

    for c in final + last:
        c.wait()


def on_device(
    query_rows, key_rows, value_rows, output_grad, output_rows, row_logsumexp,
    chosen_owner, chosen_cubes,
):
    heads = lax.axis_size("head")
    seqs = lax.axis_size("seq")
    piece_rows, full = query_rows.shape[2:]
    width = full // heads
    cubes, sel = chosen_owner.shape
    tokens = row_logsumexp.shape[0]
    rows = tokens // cubes
    piece = piece_rows // rows
    wide = CAP * rows

    def cubed(a):
        return a.reshape(piece, rows, full)

    log2 = row_logsumexp.reshape(cubes, rows) * LOG2E
    log2 = jnp.concatenate([log2] * CAP, axis=1)
    lm = jnp.where(
        chosen_cubes[:, :, :, None] != 0, log2[:, None, None, :], jnp.inf
    ).reshape(cubes * sel, cubes, wide)

    bf, f32, i32 = jnp.bfloat16, jnp.float32, jnp.int32
    vmem = pl.BlockSpec(memory_space=pltpu.VMEM)
    smem = pl.BlockSpec(memory_space=pltpu.SMEM)
    dma = pltpu.SemaphoreType.DMA
    tok = pltpu.VMEM((cubes, rows, width), bf)
    outs = pl.pallas_call(
        functools.partial(kernel, heads, seqs, sel),
        out_shape=[jax.ShapeDtypeStruct((piece, rows, full), bf)] * 3,
        in_specs=[smem] + [vmem] * 6,
        out_specs=[vmem] * 3,
        scratch_shapes=[
            tok, tok, tok, tok,
            pltpu.VMEM((width, cubes * rows), bf),
            pltpu.VMEM((heads, piece, 8, wide), f32),
            pltpu.VMEM((cubes, 8, wide), f32),
            pltpu.VMEM((cubes * sel + 1, 8, wide), f32),
            pltpu.SMEM((seqs * CAP,), i32),
            pltpu.SMEM((seqs * CAP,), i32),
            pltpu.SMEM((cubes * sel,), i32),
            pltpu.VMEM((seqs, 2, wide, width), bf),
            pltpu.VMEM((seqs, 2, wide, width), bf),
            pltpu.VMEM((seqs, 16, wide), f32),
            pltpu.VMEM((seqs, 16, wide), f32),
            pltpu.VMEM((cubes * rows, width), f32),
            pltpu.VMEM((cubes * rows, width), f32),
            tok, tok, tok,
            pltpu.VMEM((seqs, CAP, rows, width), bf),
            pltpu.VMEM((seqs * CAP, rows, width), bf),
            dma((7,)),
            dma((heads, 5)), dma((heads, 5)),
            dma((seqs,)), dma((seqs,)), dma((seqs,)), dma((seqs,)),
            dma((seqs,)), dma((seqs,)),
            dma((heads, 3)), dma((heads, 3)),
        ],
        compiler_params=pltpu.CompilerParams(collective_id=0, has_side_effects=True),
    )(
        chosen_owner.reshape(-1), cubed(query_rows), cubed(key_rows), cubed(value_rows),
        cubed(output_grad), cubed(output_rows), lm,
    )
    return tuple(a.reshape(1, 1, piece_rows, full) for a in outs)


def solution(mesh):
    rows = P("seq", "head", None, None)
    return jax.shard_map(
        on_device,
        mesh=mesh,
        in_specs=(rows, rows, rows, rows, rows, P("seq", "head"), P("seq", None), P("seq", None, None)),
        out_specs=(rows, rows, rows),
        check_vma=False,
    )
```

```python
import functools
import math

import jax
import jax.numpy as jnp
from jax import lax
from jax.experimental import pallas as pl
from jax.experimental.pallas import tpu as pltpu
from jax.sharding import PartitionSpec as P

CAP = 2
LOG2E = math.log2(math.e)
NT = (((1,), (1,)), ((), ()))
NN = (((1,), (0,)), ((), ()))


def kernel(
    heads, seqs, sel,
    owner_ref, table_ref, q_ref, k_ref, v_ref, g_ref, o_ref, lse_ref,
    oq_ref, ok_ref, ov_ref,
    qh, gh, kh, vh, kt, dsend, dlt, lz, tab_x, tab_m, ret_ix,
    fown, fown_s, fq, fg, fmeta, cmeta, ftab, fqd,
    sqd, rqd, smeta, rmeta, dk, dv, gq, gk, gv, sret, ret,
    loc_sem, hs_sem, hr_sem, xs_sem, xr_sem, ds_sem, dr_sem, ms_sem, mr_sem,
    rs_sem, rr_sem, os_sem, or_sem,
):
    me_h = lax.axis_index("head")
    me_s = lax.axis_index("seq")
    cubes, rows, width = qh.shape
    piece = q_ref.shape[0]
    pairs = cubes * sel
    scale = 1.0 / math.sqrt(width)
    half = seqs // 2
    wide = CAP * rows
    keys = cubes * rows
    metas = dlt.shape[1]

    def mate(i):
        d = me_s
        for b in range(seqs.bit_length() - 1):
            w = 1 << b
            d = d + ((i // w) % 2) * w * (1 - 2 * ((me_s // w) % 2))
        return d

    far = mate(half)

    barrier = pltpu.get_barrier_semaphore()
    for t in range(1, heads):
        pl.semaphore_signal(barrier, inc=1, device_id={"head": (me_h + t) % heads, "seq": me_s})

    @pl.loop(1, seqs)
    def _(i):
        pl.semaphore_signal(barrier, inc=1, device_id={"head": me_h, "seq": mate(i)})

    def cols(h):
        return pl.ds(pl.multiple_of(h * width, width), width)

    def rows_of(h):
        return pl.ds(h * piece, piece)

    srcs = (q_ref, g_ref, k_ref, v_ref)
    dsts = (qh, gh, kh, vh)
    own = [
        pltpu.make_async_copy(s.at[:, :, cols(me_h)], d.at[rows_of(me_h)], loc_sem.at[n])
        for n, (s, d) in enumerate(zip(srcs, dsts))
    ]
    for c in own:
        c.start()

    row = lax.broadcasted_iota(jnp.int32, (metas, wide), 0)
    lane = lax.broadcasted_iota(jnp.int32, (metas, wide), 1)
    for a in range(heads):
        for x in range(piece):
            prod = g_ref[x, :, a * width:(a + 1) * width].astype(jnp.float32) * o_ref[
                x, :, a * width:(a + 1) * width
            ].astype(jnp.float32)
            both = jnp.concatenate([prod] * CAP, axis=0)
            line = jnp.sum(both.T, axis=0, keepdims=True)
            dsend[a, x] = jnp.where(row == 1, jnp.broadcast_to(line, (metas, wide)), 0.0)
    for x in range(cubes):
        line = jnp.concatenate([lse_ref[:, x * rows:(x + 1) * rows] * LOG2E] * CAP, axis=1)
        lz[x] = jnp.where(row == 0, jnp.broadcast_to(line, (metas, wide)), 0.0)

    pl.semaphore_wait(barrier, heads - 1 + seqs - 1)

    def head_copy(t, n):
        to = (me_h + t) % heads
        if n == 4:
            src, dst = dsend.at[to], dlt.at[rows_of(me_h)]
        else:
            src, dst = srcs[n].at[:, :, cols(to)], dsts[n].at[rows_of(me_h)]
        return pltpu.make_async_remote_copy(
            src_ref=src, dst_ref=dst, send_sem=hs_sem.at[t, n], recv_sem=hr_sem.at[t, n],
            device_id={"head": to, "seq": me_s})

    def far_copy(n, src, dst):
        return pltpu.make_async_remote_copy(
            src_ref=src, dst_ref=dst, send_sem=xs_sem.at[n], recv_sem=xr_sem.at[n],
            device_id={"head": me_h, "seq": far})

    def far_part(n, t):
        h = (me_h + heads - t) % heads
        src = srcs[n].at[:, :, cols(me_h)] if t == 0 else dsts[n].at[rows_of(h)]
        return far_copy(2 + n * heads + t, src, (fq, fg)[n].at[rows_of(h)])

    owners = far_copy(0, table_ref, fown)
    far_meta = far_copy(1, cmeta, fmeta)

    owners.start()
    far_part(0, 0).start()
    for n in (0, 1, 4, 2, 3):
        for t in range(1, heads):
            head_copy(t, n).start()
    dlt[rows_of(me_h)] = dsend[me_h]

    def slots_of(read, d):
        count = jnp.int32(0)
        xs = [jnp.int32(0)] * CAP
        fs = [jnp.int32(-1)] * CAP
        for x in range(cubes):
            for j in range(sel):
                hit = read(x * sel + j) == d
                for c in range(CAP):
                    take = hit & (count == c)
                    xs[c] = jnp.where(take, x, xs[c])
                    fs[c] = jnp.where(take, x * sel + j, fs[c])
                count = count + hit.astype(jnp.int32)
        return xs, fs

    @pl.loop(0, seqs)
    def _(i):
        xs, fs = slots_of(lambda f: owner_ref[f], mate(i))
        for c in range(CAP):
            bits = owner_ref[pairs + jnp.maximum(fs[c], 0)]
            tab_x[i * CAP + c] = xs[c]
            tab_m[i * CAP + c] = jnp.where(fs[c] >= 0, bits, 0)

    for t in range(1, heads):
        head_copy(t, 0).wait_recv()
        far_part(0, t).start()
    far_part(1, 0).start()
    for t in range(1, heads):
        head_copy(t, 1).wait_recv()
        far_part(1, t).start()
    for c in own[:2]:
        c.wait()
    for t in range(1, heads):
        head_copy(t, 4).wait_recv()

    def info(i):
        both = None
        for c in range(CAP):
            x = tab_x[i * CAP + c]
            bits = tab_m[i * CAP + c].astype(jnp.float32)
            one = jnp.where(row == 2, bits, dlt[x] + lz[x])
            both = one if c == 0 else jnp.where(lane < c * rows, both, one)
        return both

    @pl.loop(0, half)
    def _(i):
        cmeta[i] = info(half + i)

    far_meta.start()

    def data_copy(i):
        dev = {"head": me_h, "seq": mate(i)}
        return (
            pltpu.make_async_remote_copy(
                src_ref=sqd.at[i], dst_ref=rqd.at[i], send_sem=ds_sem.at[i],
                recv_sem=dr_sem.at[i], device_id=dev),
            pltpu.make_async_remote_copy(
                src_ref=smeta.at[i], dst_ref=rmeta.at[i], send_sem=ms_sem.at[i],
                recv_sem=mr_sem.at[i], device_id=dev),
        )

    def passed_copy(i, n):
        dev = {"head": me_h, "seq": mate(i)}
        if n == 2:
            return pltpu.make_async_remote_copy(
                src_ref=fmeta.at[i], dst_ref=rmeta.at[half + i], send_sem=ms_sem.at[half + i],
                recv_sem=mr_sem.at[half + i], device_id=dev)
        return pltpu.make_async_remote_copy(
            src_ref=fqd.at[i, n], dst_ref=rqd.at[half + i, n],
            send_sem=ds_sem.at[half + i + n * half],
            recv_sem=dr_sem.at[half + i + n * half], device_id=dev)

    def back_copy(i):
        return pltpu.make_async_remote_copy(
            src_ref=sret.at[i], dst_ref=ret.at[pl.ds(me_s * CAP, CAP)],
            send_sem=rs_sem.at[i], recv_sem=rr_sem.at[i],
            device_id={"head": me_h, "seq": mate(i)})

    def fill(i, qd, meta):
        for c in range(CAP):
            x = tab_x[i * CAP + c]
            qd[i, 0, c * rows:(c + 1) * rows] = qh[x]
            qd[i, 1, c * rows:(c + 1) * rows] = gh[x]
        meta[i] = info(i)

    @pl.loop(1, half)
    def _(i):
        fill(half - i, sqd, smeta)
        for c in data_copy(half - i):
            c.start()

    fill(0, rqd, rmeta)

    owners.wait_recv()
    to_smem = pltpu.make_async_copy(fown, fown_s, loc_sem.at[7])
    to_smem.start()
    to_smem.wait()

    @pl.loop(0, half)
    def _(i):
        xs, _ = slots_of(lambda f: fown_s[0, f], mate(i))
        for c in range(CAP):
            ftab[i * CAP + c] = xs[c]

    def pass_on(n):
        src = (fq, fg)[n]
        for t in range(heads):
            far_part(n, t).wait_recv()

        @pl.loop(1, half)
        def _(k):
            i = half - k
            for c in range(CAP):
                fqd[i, n, c * rows:(c + 1) * rows] = src[ftab[i * CAP + c]]
            passed_copy(i, n).start()

        for c in range(CAP):
            rqd[half, n, c * rows:(c + 1) * rows] = src[ftab[c]]

    pass_on(0)
    far_meta.wait_recv()

    @pl.loop(1, half)
    def _(i):
        passed_copy(i, 2).start()

    rmeta[half] = fmeta[0]

    for c in own[2:]:
        c.wait()
    for t in range(1, heads):
        head_copy(t, 2).wait_recv()
        head_copy(t, 3).wait_recv()

    kt[...] = kh[...].reshape(keys, width).astype(jnp.float32).T.astype(jnp.bfloat16)
    dk[...] = jnp.zeros_like(dk)
    dv[...] = jnp.zeros_like(dv)
    bit = lax.broadcasted_iota(jnp.int32, (cubes, 2 * wide), 0)

    def work(k):
        base = 2 * k
        qb = jnp.concatenate([rqd[base, 0], rqd[base + 1, 0]], axis=0)
        gb = jnp.concatenate([rqd[base, 1], rqd[base + 1, 1]], axis=0)
        meta = jnp.concatenate([rmeta[base], rmeta[base + 1]], axis=1)
        kept = (meta[2:3].astype(jnp.int32) >> bit) & 1
        line = jnp.where(kept == 1, meta[0:1], jnp.inf)
        kk = kh[...].reshape(keys, width)
        vv = vh[...].reshape(keys, width)
        st = lax.dot_general(kk, qb, NT, preferred_element_type=jnp.float32)
        dpt = lax.dot_general(vv, gb, NT, preferred_element_type=jnp.float32)
        st = st.reshape(cubes, rows, 2 * wide)
        p = jnp.exp2(st * (scale * LOG2E) - line[:, None, :])
        ds = p * (dpt.reshape(cubes, rows, 2 * wide) - meta[1:2][:, None, :])
        pb = p.astype(jnp.bfloat16).reshape(keys, 2 * wide)
        dsb = ds.astype(jnp.bfloat16).reshape(keys, 2 * wide)
        dv[...] += lax.dot_general(pb, gb, NN, preferred_element_type=jnp.float32)
        dk[...] += lax.dot_general(dsb, qb, NN, preferred_element_type=jnp.float32)
        dqt = lax.dot_general(kt[...], dsb, NN, preferred_element_type=jnp.float32)
        dq = (dqt.T * scale).astype(jnp.bfloat16)
        return dq.reshape(2, CAP, rows, width)

    def near_in(i):
        for c in data_copy(i):
            c.wait_recv()

    def far_in(i):
        for n in range(3):
            passed_copy(i, n).wait_recv()

    def give(i, dq):
        sret[i] = dq
        back_copy(i).start()

    near_in(1)
    dq = work(0)
    ret[pl.ds(me_s * CAP, CAP)] = dq[0]
    give(1, dq[1])

    @pl.loop(1, half // 2)
    def _(k):
        near_in(2 * k)
        near_in(2 * k + 1)
        dq = work(k)
        give(2 * k, dq[0])
        give(2 * k + 1, dq[1])

    pass_on(1)

    far_in(1)
    dq = work(half // 2)
    give(half, dq[0])
    give(half + 1, dq[1])

    @pl.loop(1, half // 2)
    def _(k):
        far_in(2 * k)
        far_in(2 * k + 1)
        dq = work(half // 2 + k)
        give(half + 2 * k, dq[0])
        give(half + 2 * k + 1, dq[1])

    gk[...] = (dk[...] * scale).astype(jnp.bfloat16).reshape(gk.shape)
    gv[...] = dv[...].astype(jnp.bfloat16).reshape(gv.shape)
    grads, outs = (gk, gv, gq), (ok_ref, ov_ref, oq_ref)

    def out_copies(n):
        remote = []
        for t in range(1, heads):
            to = (me_h + t) % heads
            remote.append(pltpu.make_async_remote_copy(
                src_ref=grads[n].at[rows_of(to)], dst_ref=outs[n].at[:, :, cols(me_h)],
                send_sem=os_sem.at[t, n], recv_sem=or_sem.at[t, n],
                device_id={"head": to, "seq": me_s}))
        local = pltpu.make_async_copy(
            grads[n].at[rows_of(me_h)], outs[n].at[:, :, cols(me_h)], loc_sem.at[4 + n])
        return remote + [local]

    final = out_copies(0) + out_copies(1)
    for c in final:
        c.start()

    for x in range(cubes):
        for j in range(sel):
            d = owner_ref[x * sel + j]
            before = jnp.int32(0)
            for y in range(x):
                for m in range(sel):
                    before = before + (owner_ref[y * sel + m] == d).astype(jnp.int32)
            ret_ix[x * sel + j] = d * CAP + jnp.minimum(before, CAP - 1)

    @pl.loop(1, seqs)
    def _(i):
        back_copy(i).wait_recv()

    for x in range(cubes):
        total = ret[ret_ix[x * sel]].astype(jnp.float32)
        for j in range(1, sel):
            total = total + ret[ret_ix[x * sel + j]].astype(jnp.float32)
        gq[x] = total.astype(jnp.bfloat16)
    last = out_copies(2)
    for c in last:
        c.start()

    for t in range(1, heads):
        for n in range(5):
            head_copy(t, n).wait_send()
    owners.wait_send()
    far_meta.wait_send()
    for n in range(2):
        for t in range(heads):
            far_part(n, t).wait_send()

    @pl.loop(1, half)
    def _(i):
        for c in data_copy(i):
            c.wait_send()
        for n in range(3):
            passed_copy(i, n).wait_send()

    @pl.loop(1, seqs)
    def _(i):
        back_copy(i).wait_send()

    for c in final + last:
        c.wait()


def on_device(
    query_rows, key_rows, value_rows, output_grad, output_rows, row_logsumexp,
    chosen_owner, chosen_cubes,
):
    heads = lax.axis_size("head")
    seqs = lax.axis_size("seq")
    piece_rows, full = query_rows.shape[2:]
    width = full // heads
    cubes, sel = chosen_owner.shape
    tokens = row_logsumexp.shape[0]
    rows = tokens // cubes
    piece = piece_rows // rows
    wide = CAP * rows
    half = seqs // 2

    def cubed(a):
        return a.reshape(piece, rows, full)

    weight = 1 << jnp.arange(chosen_cubes.shape[2], dtype=jnp.int32)
    bits = jnp.sum(jnp.where(chosen_cubes != 0, weight, 0), axis=2)
    table = jnp.stack([chosen_owner, bits]).reshape(-1)
    lanes = -(-chosen_owner.size // 128) * 128
    owners = jnp.pad(chosen_owner.reshape(1, -1), ((0, 0), (0, lanes - chosen_owner.size)))

    bf, f32, i32 = jnp.bfloat16, jnp.float32, jnp.int32
    vmem = pl.BlockSpec(memory_space=pltpu.VMEM)
    smem = pl.BlockSpec(memory_space=pltpu.SMEM)
    dma = pltpu.SemaphoreType.DMA
    tok = pltpu.VMEM((cubes, rows, width), bf)
    outs = pl.pallas_call(
        functools.partial(kernel, heads, seqs, sel),
        out_shape=[jax.ShapeDtypeStruct((piece, rows, full), bf)] * 3,
        in_specs=[smem] + [vmem] * 7,
        out_specs=[vmem] * 3,
        scratch_shapes=[
            tok, tok, tok, tok,
            pltpu.VMEM((width, cubes * rows), bf),
            pltpu.VMEM((heads, piece, 4, wide), f32),
            pltpu.VMEM((cubes, 4, wide), f32),
            pltpu.VMEM((cubes, 4, wide), f32),
            pltpu.SMEM((seqs * CAP,), i32),
            pltpu.SMEM((seqs * CAP,), i32),
            pltpu.SMEM((cubes * sel,), i32),
            pltpu.VMEM((1, lanes), i32),
            pltpu.SMEM((1, lanes), i32),
            tok, tok,
            pltpu.VMEM((half, 4, wide), f32),
            pltpu.VMEM((half, 4, wide), f32),
            pltpu.SMEM((half * CAP,), i32),
            pltpu.VMEM((half, 2, wide, width), bf),
            pltpu.VMEM((half, 2, wide, width), bf),
            pltpu.VMEM((seqs, 2, wide, width), bf),
            pltpu.VMEM((half, 4, wide), f32),
            pltpu.VMEM((seqs, 4, wide), f32),
            pltpu.VMEM((cubes * rows, width), f32),
            pltpu.VMEM((cubes * rows, width), f32),
            tok, tok, tok,
            pltpu.VMEM((seqs, CAP, rows, width), bf),
            pltpu.VMEM((seqs * CAP, rows, width), bf),
            dma((8,)),
            dma((heads, 5)), dma((heads, 5)),
            dma((2 + 2 * heads,)), dma((2 + 2 * heads,)),
            dma((seqs + half,)), dma((seqs + half,)), dma((seqs,)), dma((seqs,)),
            dma((seqs,)), dma((seqs,)),
            dma((heads, 3)), dma((heads, 3)),
        ],
        compiler_params=pltpu.CompilerParams(collective_id=0, has_side_effects=True),
    )(
        table, owners, cubed(query_rows), cubed(key_rows), cubed(value_rows),
        cubed(output_grad), cubed(output_rows),
        row_logsumexp.reshape(1, tokens),
    )
    return tuple(a.reshape(1, 1, piece_rows, full) for a in outs)


def solution(mesh):
    rows = P("seq", "head", None, None)
    return jax.shard_map(
        on_device,
        mesh=mesh,
        in_specs=(rows, rows, rows, rows, rows, P("seq", "head"), P("seq", None), P("seq", None, None)),
        out_specs=(rows, rows, rows),
        check_vma=False,
    )
```

```python
import functools
import math

import jax
import jax.numpy as jnp
from jax import lax
from jax.experimental import pallas as pl
from jax.experimental.pallas import tpu as pltpu
from jax.sharding import PartitionSpec as P

CAP = 2
LOG2E = math.log2(math.e)
NT = (((1,), (1,)), ((), ()))
NN = (((1,), (0,)), ((), ()))


def kernel(
    heads, seqs, sel,
    owner_ref, pick_ref, table_ref, q_ref, k_ref, v_ref, g_ref, o_ref, lse_ref,
    oq_ref, ok_ref, ov_ref,
    qh, gh, kh, vh, kt, g_all, o_all, dsend, dlt, lz, bits_of, tab_x, tab_m, ret_ix,
    fown, fown_s, fq, fg, fmeta, cmeta, ftab, fqd,
    sqd, rqd, smeta, rmeta, dk, dv, gq, gk, gv, sret, ret,
    loc_sem, hs_sem, hr_sem, xs_sem, xr_sem, ds_sem, dr_sem, ms_sem, mr_sem,
    rs_sem, rr_sem, os_sem, or_sem,
):
    me_h = lax.axis_index("head")
    me_s = lax.axis_index("seq")
    cubes, rows, width = qh.shape
    piece = q_ref.shape[0]
    scale = 1.0 / math.sqrt(width)
    half = seqs // 2
    wide = CAP * rows
    keys = cubes * rows
    metas = dlt.shape[1]

    def mate(i):
        d = me_s
        for b in range(seqs.bit_length() - 1):
            w = 1 << b
            d = d + ((i // w) % 2) * w * (1 - 2 * ((me_s // w) % 2))
        return d

    far = mate(half)

    barrier = pltpu.get_barrier_semaphore()
    for t in range(1, heads):
        pl.semaphore_signal(barrier, inc=1, device_id={"head": (me_h + t) % heads, "seq": me_s})

    @pl.loop(1, seqs)
    def _(i):
        pl.semaphore_signal(barrier, inc=1, device_id={"head": me_h, "seq": mate(i)})

    def cols(h):
        return pl.ds(pl.multiple_of(h * width, width), width)

    def rows_of(h):
        return pl.ds(h * piece, piece)

    srcs = (q_ref, g_ref, k_ref, v_ref)
    dsts = (qh, gh, kh, vh)
    own = [
        pltpu.make_async_copy(s.at[:, :, cols(me_h)], d.at[rows_of(me_h)], loc_sem.at[n])
        for n, (s, d) in enumerate(zip(srcs, dsts))
    ]
    whole = [
        pltpu.make_async_copy(s, d, loc_sem.at[8 + n])
        for n, (s, d) in enumerate(((g_ref, g_all), (o_ref, o_all)))
    ]
    for c in whole + own:
        c.start()

    for x in range(cubes):
        for j in range(sel):
            bits = jnp.int32(0)
            for k in range(cubes):
                bits = bits + jnp.where(pick_ref[x, j, k] != 0, 1 << k, 0)
            bits_of[x * sel + j] = bits

    for c in whole:
        c.wait()

    row = lax.broadcasted_iota(jnp.int32, (metas, wide), 0)
    lane = lax.broadcasted_iota(jnp.int32, (metas, wide), 1)
    for a in range(heads):
        for x in range(piece):
            prod = g_all[x, :, a * width:(a + 1) * width].astype(jnp.float32) * o_all[
                x, :, a * width:(a + 1) * width
            ].astype(jnp.float32)
            both = jnp.concatenate([prod] * CAP, axis=0)
            line = jnp.sum(both.T, axis=0, keepdims=True)
            dsend[a, x] = jnp.where(row == 1, jnp.broadcast_to(line, (metas, wide)), 0.0)
    for x in range(cubes):
        line = jnp.concatenate([lse_ref[:, x * rows:(x + 1) * rows] * LOG2E] * CAP, axis=1)
        lz[x] = jnp.where(row == 0, jnp.broadcast_to(line, (metas, wide)), 0.0)

    pl.semaphore_wait(barrier, heads - 1 + seqs - 1)

    def head_copy(t, n):
        to = (me_h + t) % heads
        if n == 4:
            src, dst = dsend.at[to], dlt.at[rows_of(me_h)]
        else:
            src, dst = srcs[n].at[:, :, cols(to)], dsts[n].at[rows_of(me_h)]
        return pltpu.make_async_remote_copy(
            src_ref=src, dst_ref=dst, send_sem=hs_sem.at[t, n], recv_sem=hr_sem.at[t, n],
            device_id={"head": to, "seq": me_s})

    def far_copy(n, src, dst):
        return pltpu.make_async_remote_copy(
            src_ref=src, dst_ref=dst, send_sem=xs_sem.at[n], recv_sem=xr_sem.at[n],
            device_id={"head": me_h, "seq": far})

    def far_part(n, t):
        h = (me_h + heads - t) % heads
        src = srcs[n].at[:, :, cols(me_h)] if t == 0 else dsts[n].at[rows_of(h)]
        return far_copy(2 + n * heads + t, src, (fq, fg)[n].at[rows_of(h)])

    owners = far_copy(0, table_ref, fown)
    far_meta = far_copy(1, cmeta, fmeta)

    owners.start()
    far_part(0, 0).start()
    for n in (0, 1, 4, 2, 3):
        for t in range(1, heads):
            head_copy(t, n).start()
    dlt[rows_of(me_h)] = dsend[me_h]

    def slots_of(read, d):
        count = jnp.int32(0)
        xs = [jnp.int32(0)] * CAP
        fs = [jnp.int32(-1)] * CAP
        for x in range(cubes):
            for j in range(sel):
                hit = read(x, j) == d
                for c in range(CAP):
                    take = hit & (count == c)
                    xs[c] = jnp.where(take, x, xs[c])
                    fs[c] = jnp.where(take, x * sel + j, fs[c])
                count = count + hit.astype(jnp.int32)
        return xs, fs

    @pl.loop(0, seqs)
    def _(i):
        xs, fs = slots_of(lambda x, j: owner_ref[j, x], mate(i))
        for c in range(CAP):
            bits = bits_of[jnp.maximum(fs[c], 0)]
            tab_x[i * CAP + c] = xs[c]
            tab_m[i * CAP + c] = jnp.where(fs[c] >= 0, bits, 0)

    for t in range(1, heads):
        head_copy(t, 0).wait_recv()
        far_part(0, t).start()
    far_part(1, 0).start()
    for t in range(1, heads):
        head_copy(t, 1).wait_recv()
        far_part(1, t).start()
    for c in own[:2]:
        c.wait()
    for t in range(1, heads):
        head_copy(t, 4).wait_recv()

    def info(i):
        both = None
        for c in range(CAP):
            x = tab_x[i * CAP + c]
            bits = tab_m[i * CAP + c].astype(jnp.float32)
            one = jnp.where(row == 2, bits, dlt[x] + lz[x])
            both = one if c == 0 else jnp.where(lane < c * rows, both, one)
        return both

    @pl.loop(0, half)
    def _(i):
        cmeta[i] = info(half + i)

    far_meta.start()

    def data_copy(i):
        dev = {"head": me_h, "seq": mate(i)}
        return (
            pltpu.make_async_remote_copy(
                src_ref=sqd.at[i], dst_ref=rqd.at[i], send_sem=ds_sem.at[i],
                recv_sem=dr_sem.at[i], device_id=dev),
            pltpu.make_async_remote_copy(
                src_ref=smeta.at[i], dst_ref=rmeta.at[i], send_sem=ms_sem.at[i],
                recv_sem=mr_sem.at[i], device_id=dev),
        )

    def passed_copy(i, n):
        dev = {"head": me_h, "seq": mate(i)}
        if n == 2:
            return pltpu.make_async_remote_copy(
                src_ref=fmeta.at[i], dst_ref=rmeta.at[half + i], send_sem=ms_sem.at[half + i],
                recv_sem=mr_sem.at[half + i], device_id=dev)
        return pltpu.make_async_remote_copy(
            src_ref=fqd.at[i, n], dst_ref=rqd.at[half + i, n],
            send_sem=ds_sem.at[half + i + n * half],
            recv_sem=dr_sem.at[half + i + n * half], device_id=dev)

    def back_copy(i):
        return pltpu.make_async_remote_copy(
            src_ref=sret.at[i], dst_ref=ret.at[pl.ds(me_s * CAP, CAP)],
            send_sem=rs_sem.at[i], recv_sem=rr_sem.at[i],
            device_id={"head": me_h, "seq": mate(i)})

    def fill(i, qd, meta):
        for c in range(CAP):
            x = tab_x[i * CAP + c]
            qd[i, 0, c * rows:(c + 1) * rows] = qh[x]
            qd[i, 1, c * rows:(c + 1) * rows] = gh[x]
        meta[i] = info(i)

    @pl.loop(1, half)
    def _(i):
        fill(half - i, sqd, smeta)
        for c in data_copy(half - i):
            c.start()

    fill(0, rqd, rmeta)

    owners.wait_recv()
    to_smem = pltpu.make_async_copy(fown, fown_s, loc_sem.at[7])
    to_smem.start()
    to_smem.wait()

    @pl.loop(0, half)
    def _(i):
        xs, _ = slots_of(lambda x, j: fown_s[j, x], mate(i))
        for c in range(CAP):
            ftab[i * CAP + c] = xs[c]

    def pass_on(n):
        src = (fq, fg)[n]
        for t in range(heads):
            far_part(n, t).wait_recv()

        @pl.loop(1, half)
        def _(k):
            i = half - k
            for c in range(CAP):
                fqd[i, n, c * rows:(c + 1) * rows] = src[ftab[i * CAP + c]]
            passed_copy(i, n).start()

        for c in range(CAP):
            rqd[half, n, c * rows:(c + 1) * rows] = src[ftab[c]]

    pass_on(0)
    far_meta.wait_recv()

    @pl.loop(1, half)
    def _(i):
        passed_copy(i, 2).start()

    rmeta[half] = fmeta[0]

    for c in own[2:]:
        c.wait()
    for t in range(1, heads):
        head_copy(t, 2).wait_recv()
        head_copy(t, 3).wait_recv()

    kt[...] = kh[...].reshape(keys, width).astype(jnp.float32).T.astype(jnp.bfloat16)
    dk[...] = jnp.zeros_like(dk)
    dv[...] = jnp.zeros_like(dv)
    bit = lax.broadcasted_iota(jnp.int32, (cubes, 2 * wide), 0)

    def work(k):
        base = 2 * k
        qb = jnp.concatenate([rqd[base, 0], rqd[base + 1, 0]], axis=0)
        gb = jnp.concatenate([rqd[base, 1], rqd[base + 1, 1]], axis=0)
        meta = jnp.concatenate([rmeta[base], rmeta[base + 1]], axis=1)
        kept = (meta[2:3].astype(jnp.int32) >> bit) & 1
        line = jnp.where(kept == 1, meta[0:1], jnp.inf)
        kk = kh[...].reshape(keys, width)
        vv = vh[...].reshape(keys, width)
        st = lax.dot_general(kk, qb, NT, preferred_element_type=jnp.float32)
        dpt = lax.dot_general(vv, gb, NT, preferred_element_type=jnp.float32)
        st = st.reshape(cubes, rows, 2 * wide)
        p = jnp.exp2(st * (scale * LOG2E) - line[:, None, :])
        ds = p * (dpt.reshape(cubes, rows, 2 * wide) - meta[1:2][:, None, :])
        pb = p.astype(jnp.bfloat16).reshape(keys, 2 * wide)
        dsb = ds.astype(jnp.bfloat16).reshape(keys, 2 * wide)
        dv[...] += lax.dot_general(pb, gb, NN, preferred_element_type=jnp.float32)
        dk[...] += lax.dot_general(dsb, qb, NN, preferred_element_type=jnp.float32)
        dqt = lax.dot_general(kt[...], dsb, NN, preferred_element_type=jnp.float32)
        dq = (dqt.T * scale).astype(jnp.bfloat16)
        return dq.reshape(2, CAP, rows, width)

    def near_in(i):
        for c in data_copy(i):
            c.wait_recv()

    def far_in(i):
        for n in range(3):
            passed_copy(i, n).wait_recv()

    def give(i, dq):
        sret[i] = dq
        back_copy(i).start()

    near_in(1)
    dq = work(0)
    ret[pl.ds(me_s * CAP, CAP)] = dq[0]
    give(1, dq[1])

    @pl.loop(1, half // 2)
    def _(k):
        near_in(2 * k)
        near_in(2 * k + 1)
        dq = work(k)
        give(2 * k, dq[0])
        give(2 * k + 1, dq[1])

    pass_on(1)

    far_in(1)
    dq = work(half // 2)
    give(half, dq[0])
    give(half + 1, dq[1])

    @pl.loop(1, half // 2)
    def _(k):
        far_in(2 * k)
        far_in(2 * k + 1)
        dq = work(half // 2 + k)
        give(half + 2 * k, dq[0])
        give(half + 2 * k + 1, dq[1])

    gk[...] = (dk[...] * scale).astype(jnp.bfloat16).reshape(gk.shape)
    gv[...] = dv[...].astype(jnp.bfloat16).reshape(gv.shape)
    grads, outs = (gk, gv, gq), (ok_ref, ov_ref, oq_ref)

    def out_copies(n):
        remote = []
        for t in range(1, heads):
            to = (me_h + t) % heads
            remote.append(pltpu.make_async_remote_copy(
                src_ref=grads[n].at[rows_of(to)], dst_ref=outs[n].at[:, :, cols(me_h)],
                send_sem=os_sem.at[t, n], recv_sem=or_sem.at[t, n],
                device_id={"head": to, "seq": me_s}))
        local = pltpu.make_async_copy(
            grads[n].at[rows_of(me_h)], outs[n].at[:, :, cols(me_h)], loc_sem.at[4 + n])
        return remote + [local]

    final = out_copies(0) + out_copies(1)
    for c in final:
        c.start()

    for x in range(cubes):
        for j in range(sel):
            d = owner_ref[j, x]
            before = jnp.int32(0)
            for y in range(x):
                for m in range(sel):
                    before = before + (owner_ref[m, y] == d).astype(jnp.int32)
            ret_ix[x * sel + j] = d * CAP + jnp.minimum(before, CAP - 1)

    @pl.loop(1, seqs)
    def _(i):
        back_copy(i).wait_recv()

    for x in range(cubes):
        total = ret[ret_ix[x * sel]].astype(jnp.float32)
        for j in range(1, sel):
            total = total + ret[ret_ix[x * sel + j]].astype(jnp.float32)
        gq[x] = total.astype(jnp.bfloat16)
    last = out_copies(2)
    for c in last:
        c.start()

    for t in range(1, heads):
        for n in range(5):
            head_copy(t, n).wait_send()
    owners.wait_send()
    far_meta.wait_send()
    for n in range(2):
        for t in range(heads):
            far_part(n, t).wait_send()

    @pl.loop(1, half)
    def _(i):
        for c in data_copy(i):
            c.wait_send()
        for n in range(3):
            passed_copy(i, n).wait_send()

    @pl.loop(1, seqs)
    def _(i):
        back_copy(i).wait_send()

    for c in final + last:
        c.wait()


def place(a_ref, b_ref, c_ref, x_ref, y_ref, z_ref, sem):
    copies = [
        pltpu.make_async_copy(s, d, sem.at[n])
        for n, (s, d) in enumerate(((a_ref, x_ref), (b_ref, y_ref), (c_ref, z_ref)))
    ]
    for c in copies:
        c.start()
    for c in copies:
        c.wait()


def on_device(
    query_rows, key_rows, value_rows, output_grad, output_rows, row_logsumexp,
    chosen_owner, chosen_cubes,
):
    heads = lax.axis_size("head")
    seqs = lax.axis_size("seq")
    piece_rows, full = query_rows.shape[2:]
    width = full // heads
    cubes, sel = chosen_owner.shape
    tokens = row_logsumexp.shape[0]
    rows = tokens // cubes
    piece = piece_rows // rows
    wide = CAP * rows
    half = seqs // 2

    def cubed(a):
        return a.reshape(piece, rows, full)

    bf, f32, i32 = jnp.bfloat16, jnp.float32, jnp.int32
    vmem = pl.BlockSpec(memory_space=pltpu.VMEM)
    anywhere = pl.BlockSpec(memory_space=pl.ANY)
    smem = pl.BlockSpec(memory_space=pltpu.SMEM)
    dma = pltpu.SemaphoreType.DMA
    tok = pltpu.VMEM((cubes, rows, width), bf)
    outs = pl.pallas_call(
        functools.partial(kernel, heads, seqs, sel),
        out_shape=[jax.ShapeDtypeStruct((piece, rows, full), bf)] * 3,
        in_specs=[smem, smem, vmem] + [anywhere] * 5 + [vmem],
        out_specs=[anywhere] * 3,
        scratch_shapes=[
            tok, tok, tok, tok,
            pltpu.VMEM((width, cubes * rows), bf),
            pltpu.VMEM((piece, rows, full), bf),
            pltpu.VMEM((piece, rows, full), bf),
            pltpu.VMEM((heads, piece, 4, wide), f32),
            pltpu.VMEM((cubes, 4, wide), f32),
            pltpu.VMEM((cubes, 4, wide), f32),
            pltpu.SMEM((cubes * sel,), i32),
            pltpu.SMEM((seqs * CAP,), i32),
            pltpu.SMEM((seqs * CAP,), i32),
            pltpu.SMEM((cubes * sel,), i32),
            pltpu.VMEM((sel, cubes), i32),
            pltpu.SMEM((sel, cubes), i32),
            tok, tok,
            pltpu.VMEM((half, 4, wide), f32),
            pltpu.VMEM((half, 4, wide), f32),
            pltpu.SMEM((half * CAP,), i32),
            pltpu.VMEM((half, 2, wide, width), bf),
            pltpu.VMEM((half, 2, wide, width), bf),
            pltpu.VMEM((seqs, 2, wide, width), bf),
            pltpu.VMEM((half, 4, wide), f32),
            pltpu.VMEM((seqs, 4, wide), f32),
            pltpu.VMEM((cubes * rows, width), f32),
            pltpu.VMEM((cubes * rows, width), f32),
            tok, tok, tok,
            pltpu.VMEM((seqs, CAP, rows, width), bf),
            pltpu.VMEM((seqs * CAP, rows, width), bf),
            dma((10,)),
            dma((heads, 5)), dma((heads, 5)),
            dma((2 + 2 * heads,)), dma((2 + 2 * heads,)),
            dma((seqs + half,)), dma((seqs + half,)), dma((seqs,)), dma((seqs,)),
            dma((seqs,)), dma((seqs,)),
            dma((heads, 3)), dma((heads, 3)),
        ],
        compiler_params=pltpu.CompilerParams(collective_id=0, has_side_effects=True),
    )(
        chosen_owner.T, chosen_cubes, chosen_owner.T, cubed(query_rows), cubed(key_rows), cubed(value_rows),
        cubed(output_grad), cubed(output_rows),
        row_logsumexp.reshape(1, tokens),
    )
    outs = pl.pallas_call(
        place,
        out_shape=[jax.ShapeDtypeStruct((piece, rows, full), bf)] * 3,
        in_specs=[anywhere] * 3,
        out_specs=[vmem] * 3,
        scratch_shapes=[dma((3,))],
    )(*outs)
    return tuple(a.reshape(1, 1, piece_rows, full) for a in outs)


def solution(mesh):
    rows = P("seq", "head", None, None)
    return jax.shard_map(
        on_device,
        mesh=mesh,
        in_specs=(rows, rows, rows, rows, rows, P("seq", "head"), P("seq", None), P("seq", None, None)),
        out_specs=(rows, rows, rows),
        check_vma=False,
    )
```

```python
import functools
import math

import jax
import jax.numpy as jnp
from jax import lax
from jax.experimental import pallas as pl
from jax.experimental.pallas import tpu as pltpu
from jax.sharding import PartitionSpec as P

CAP = 2
LOG2E = math.log2(math.e)
NT = (((1,), (1,)), ((), ()))
NN = (((1,), (0,)), ((), ()))


def kernel(
    heads, seqs, sel,
    owner_ref, pick_ref, table_ref, q_ref, k_ref, v_ref, g_ref, o_ref, lse_ref,
    oq_ref, ok_ref, ov_ref,
    qh, gh, kh, vh, kt, g_all, o_all, dsend, dlt, lz, bits_of, tab_x, tab_m, ret_ix,
    fown, fown_s, fq, fg, fmeta, cmeta, ftab, fqd,
    sqd, rqd, smeta, rmeta, dk, dv, gq, gk, gv, sret, ret,
    loc_sem, hs_sem, hr_sem, xs_sem, xr_sem, ds_sem, dr_sem, ms_sem, mr_sem,
    rs_sem, rr_sem, os_sem, or_sem,
):
    me_h = lax.axis_index("head")
    me_s = lax.axis_index("seq")
    cubes, rows, width = qh.shape
    piece = q_ref.shape[0]
    scale = 1.0 / math.sqrt(width)
    half = seqs // 2
    wide = CAP * rows
    keys = cubes * rows
    metas = dlt.shape[1]

    def mate(i):
        d = me_s
        for b in range(seqs.bit_length() - 1):
            w = 1 << b
            d = d + ((i // w) % 2) * w * (1 - 2 * ((me_s // w) % 2))
        return d

    far = mate(half)

    barrier = pltpu.get_barrier_semaphore()
    for t in range(1, heads):
        pl.semaphore_signal(barrier, inc=1, device_id={"head": (me_h + t) % heads, "seq": me_s})

    @pl.loop(1, half + 1)
    def _(i):
        pl.semaphore_signal(barrier, inc=1, device_id={"head": me_h, "seq": mate(i)})

    def cols(h):
        return pl.ds(pl.multiple_of(h * width, width), width)

    def rows_of(h):
        return pl.ds(h * piece, piece)

    srcs = (q_ref, g_ref, k_ref, v_ref)
    dsts = (qh, gh, kh, vh)
    own = [
        pltpu.make_async_copy(s.at[:, :, cols(me_h)], d.at[rows_of(me_h)], loc_sem.at[n])
        for n, (s, d) in enumerate(zip(srcs, dsts))
    ]
    whole = [
        pltpu.make_async_copy(s, d, loc_sem.at[8 + n])
        for n, (s, d) in enumerate(((g_ref, g_all), (o_ref, o_all)))
    ]
    for c in whole + own:
        c.start()

    for x in range(cubes):
        for j in range(sel):
            bits = jnp.int32(0)
            for k in range(cubes):
                bits = bits + jnp.where(pick_ref[x, j, k] != 0, 1 << k, 0)
            bits_of[x * sel + j] = bits

    for c in whole:
        c.wait()

    row = lax.broadcasted_iota(jnp.int32, (metas, wide), 0)
    lane = lax.broadcasted_iota(jnp.int32, (metas, wide), 1)
    for a in range(heads):
        for x in range(piece):
            prod = g_all[x, :, a * width:(a + 1) * width].astype(jnp.float32) * o_all[
                x, :, a * width:(a + 1) * width
            ].astype(jnp.float32)
            both = jnp.concatenate([prod] * CAP, axis=0)
            line = jnp.sum(both.T, axis=0, keepdims=True)
            dsend[a, x] = jnp.where(row == 1, jnp.broadcast_to(line, (metas, wide)), 0.0)
    for x in range(cubes):
        line = jnp.concatenate([lse_ref[:, x * rows:(x + 1) * rows] * LOG2E] * CAP, axis=1)
        lz[x] = jnp.where(row == 0, jnp.broadcast_to(line, (metas, wide)), 0.0)

    pl.semaphore_wait(barrier, heads - 1 + half)

    def head_copy(t, n):
        to = (me_h + t) % heads
        if n == 4:
            src, dst = dsend.at[to], dlt.at[rows_of(me_h)]
        else:
            src, dst = srcs[n].at[:, :, cols(to)], dsts[n].at[rows_of(me_h)]
        return pltpu.make_async_remote_copy(
            src_ref=src, dst_ref=dst, send_sem=hs_sem.at[t, n], recv_sem=hr_sem.at[t, n],
            device_id={"head": to, "seq": me_s})

    def far_copy(n, src, dst):
        return pltpu.make_async_remote_copy(
            src_ref=src, dst_ref=dst, send_sem=xs_sem.at[n], recv_sem=xr_sem.at[n],
            device_id={"head": me_h, "seq": far})

    def far_part(n, t):
        h = (me_h + heads - t) % heads
        src = srcs[n].at[:, :, cols(me_h)] if t == 0 else dsts[n].at[rows_of(h)]
        return far_copy(2 + n * heads + t, src, (fq, fg)[n].at[rows_of(h)])

    owners = far_copy(0, table_ref, fown)
    far_meta = far_copy(1, cmeta, fmeta)

    owners.start()
    far_part(0, 0).start()
    far_part(1, 0).start()
    for n in (0, 1, 4, 2, 3):
        for t in range(1, heads):
            head_copy(t, n).start()
    dlt[rows_of(me_h)] = dsend[me_h]

    def slots_of(read, d):
        count = jnp.int32(0)
        xs = [jnp.int32(0)] * CAP
        fs = [jnp.int32(-1)] * CAP
        for x in range(cubes):
            for j in range(sel):
                hit = read(x, j) == d
                for c in range(CAP):
                    take = hit & (count == c)
                    xs[c] = jnp.where(take, x, xs[c])
                    fs[c] = jnp.where(take, x * sel + j, fs[c])
                count = count + hit.astype(jnp.int32)
        return xs, fs

    @pl.loop(0, seqs)
    def _(i):
        xs, fs = slots_of(lambda x, j: owner_ref[j, x], mate(i))
        for c in range(CAP):
            bits = bits_of[jnp.maximum(fs[c], 0)]
            tab_x[i * CAP + c] = xs[c]
            tab_m[i * CAP + c] = jnp.where(fs[c] >= 0, bits, 0)

    for t in range(1, heads):
        head_copy(t, 0).wait_recv()
        far_part(0, t).start()
    for t in range(1, heads):
        head_copy(t, 1).wait_recv()
        far_part(1, t).start()
    for c in own[:2]:
        c.wait()
    for t in range(1, heads):
        head_copy(t, 4).wait_recv()

    def info(i):
        both = None
        for c in range(CAP):
            x = tab_x[i * CAP + c]
            bits = tab_m[i * CAP + c].astype(jnp.float32)
            one = jnp.where(row == 2, bits, dlt[x] + lz[x])
            both = one if c == 0 else jnp.where(lane < c * rows, both, one)
        return both

    @pl.loop(0, half)
    def _(i):
        cmeta[i] = info(half + i)

    far_meta.start()

    def data_copy(i):
        dev = {"head": me_h, "seq": mate(i)}
        return (
            pltpu.make_async_remote_copy(
                src_ref=sqd.at[i], dst_ref=rqd.at[i], send_sem=ds_sem.at[i],
                recv_sem=dr_sem.at[i], device_id=dev),
            pltpu.make_async_remote_copy(
                src_ref=smeta.at[i], dst_ref=rmeta.at[i], send_sem=ms_sem.at[i],
                recv_sem=mr_sem.at[i], device_id=dev),
        )

    def passed_copy(i, n):
        dev = {"head": me_h, "seq": mate(i)}
        if n == 2:
            return pltpu.make_async_remote_copy(
                src_ref=fmeta.at[i], dst_ref=rmeta.at[half + i], send_sem=ms_sem.at[half + i],
                recv_sem=mr_sem.at[half + i], device_id=dev)
        return pltpu.make_async_remote_copy(
            src_ref=fqd.at[i, n], dst_ref=rqd.at[half + i, n],
            send_sem=ds_sem.at[half + i + n * half],
            recv_sem=dr_sem.at[half + i + n * half], device_id=dev)

    def back_copy(i):
        return pltpu.make_async_remote_copy(
            src_ref=sret.at[i], dst_ref=ret.at[pl.ds(me_s * CAP, CAP)],
            send_sem=rs_sem.at[i], recv_sem=rr_sem.at[i],
            device_id={"head": me_h, "seq": mate(i)})

    def fill(i, qd, meta):
        for c in range(CAP):
            x = tab_x[i * CAP + c]
            qd[i, 0, c * rows:(c + 1) * rows] = qh[x]
            qd[i, 1, c * rows:(c + 1) * rows] = gh[x]
        meta[i] = info(i)

    @pl.loop(1, half)
    def _(i):
        fill(half - i, sqd, smeta)
        for c in data_copy(half - i):
            c.start()

    fill(0, rqd, rmeta)

    owners.wait_recv()
    to_smem = pltpu.make_async_copy(fown, fown_s, loc_sem.at[7])
    to_smem.start()
    to_smem.wait()

    @pl.loop(0, half)
    def _(i):
        xs, _ = slots_of(lambda x, j: fown_s[j, x], mate(i))
        for c in range(CAP):
            ftab[i * CAP + c] = xs[c]

    def pass_on(n):
        src = (fq, fg)[n]
        for t in range(heads):
            far_part(n, t).wait_recv()

        @pl.loop(1, half)
        def _(k):
            i = half - k
            for c in range(CAP):
                fqd[i, n, c * rows:(c + 1) * rows] = src[ftab[i * CAP + c]]
            passed_copy(i, n).start()

        for c in range(CAP):
            rqd[half, n, c * rows:(c + 1) * rows] = src[ftab[c]]

    pass_on(0)
    far_meta.wait_recv()

    @pl.loop(1, half)
    def _(i):
        passed_copy(i, 2).start()

    rmeta[half] = fmeta[0]

    for c in own[2:]:
        c.wait()
    for t in range(1, heads):
        head_copy(t, 2).wait_recv()
        head_copy(t, 3).wait_recv()

    kt[...] = kh[...].reshape(keys, width).astype(jnp.float32).T.astype(jnp.bfloat16)
    dk[...] = jnp.zeros_like(dk)
    dv[...] = jnp.zeros_like(dv)
    bit = lax.broadcasted_iota(jnp.int32, (cubes, 2 * wide), 0)

    def work(k):
        base = 2 * k
        qb = jnp.concatenate([rqd[base, 0], rqd[base + 1, 0]], axis=0)
        gb = jnp.concatenate([rqd[base, 1], rqd[base + 1, 1]], axis=0)
        meta = jnp.concatenate([rmeta[base], rmeta[base + 1]], axis=1)
        kept = (meta[2:3].astype(jnp.int32) >> bit) & 1
        line = jnp.where(kept == 1, meta[0:1], jnp.inf)
        kk = kh[...].reshape(keys, width)
        vv = vh[...].reshape(keys, width)
        st = lax.dot_general(kk, qb, NT, preferred_element_type=jnp.float32)
        dpt = lax.dot_general(vv, gb, NT, preferred_element_type=jnp.float32)
        st = st.reshape(cubes, rows, 2 * wide)
        p = jnp.exp2(st * (scale * LOG2E) - line[:, None, :])
        ds = p * (dpt.reshape(cubes, rows, 2 * wide) - meta[1:2][:, None, :])
        pb = p.astype(jnp.bfloat16).reshape(keys, 2 * wide)
        dsb = ds.astype(jnp.bfloat16).reshape(keys, 2 * wide)
        dv[...] += lax.dot_general(pb, gb, NN, preferred_element_type=jnp.float32)
        dk[...] += lax.dot_general(dsb, qb, NN, preferred_element_type=jnp.float32)
        dqt = lax.dot_general(kt[...], dsb, NN, preferred_element_type=jnp.float32)
        dq = (dqt.T * scale).astype(jnp.bfloat16)
        return dq.reshape(2, CAP, rows, width)

    def near_in(i):
        for c in data_copy(i):
            c.wait_recv()

    def far_in(i):
        for n in range(3):
            passed_copy(i, n).wait_recv()

    def give(i, dq):
        sret[i] = dq
        back_copy(i).start()

    near_in(1)
    dq = work(0)
    ret[pl.ds(me_s * CAP, CAP)] = dq[0]
    give(1, dq[1])

    @pl.loop(1, half // 2)
    def _(k):
        near_in(2 * k)
        near_in(2 * k + 1)
        dq = work(k)
        give(2 * k, dq[0])
        give(2 * k + 1, dq[1])

    pass_on(1)

    far_in(1)
    dq = work(half // 2)
    give(half, dq[0])
    give(half + 1, dq[1])

    @pl.loop(1, half // 2)
    def _(k):
        far_in(2 * k)
        far_in(2 * k + 1)
        dq = work(half // 2 + k)
        give(half + 2 * k, dq[0])
        give(half + 2 * k + 1, dq[1])

    gk[...] = (dk[...] * scale).astype(jnp.bfloat16).reshape(gk.shape)
    gv[...] = dv[...].astype(jnp.bfloat16).reshape(gv.shape)
    grads, outs = (gk, gv, gq), (ok_ref, ov_ref, oq_ref)

    def out_copies(n):
        remote = []
        for t in range(1, heads):
            to = (me_h + t) % heads
            remote.append(pltpu.make_async_remote_copy(
                src_ref=grads[n].at[rows_of(to)], dst_ref=outs[n].at[:, :, cols(me_h)],
                send_sem=os_sem.at[t, n], recv_sem=or_sem.at[t, n],
                device_id={"head": to, "seq": me_s}))
        local = pltpu.make_async_copy(
            grads[n].at[rows_of(me_h)], outs[n].at[:, :, cols(me_h)], loc_sem.at[4 + n])
        return remote + [local]

    final = out_copies(0) + out_copies(1)
    for c in final:
        c.start()

    for x in range(cubes):
        for j in range(sel):
            d = owner_ref[j, x]
            before = jnp.int32(0)
            for y in range(x):
                for m in range(sel):
                    before = before + (owner_ref[m, y] == d).astype(jnp.int32)
            ret_ix[x * sel + j] = d * CAP + jnp.minimum(before, CAP - 1)

    @pl.loop(1, seqs)
    def _(i):
        back_copy(i).wait_recv()

    for x in range(cubes):
        total = ret[ret_ix[x * sel]].astype(jnp.float32)
        for j in range(1, sel):
            total = total + ret[ret_ix[x * sel + j]].astype(jnp.float32)
        gq[x] = total.astype(jnp.bfloat16)
    last = out_copies(2)
    for c in last:
        c.start()

    for t in range(1, heads):
        for n in range(5):
            head_copy(t, n).wait_send()
    owners.wait_send()
    far_meta.wait_send()
    for n in range(2):
        for t in range(heads):
            far_part(n, t).wait_send()

    @pl.loop(1, half)
    def _(i):
        for c in data_copy(i):
            c.wait_send()
        for n in range(3):
            passed_copy(i, n).wait_send()

    @pl.loop(1, seqs)
    def _(i):
        back_copy(i).wait_send()

    for c in final + last:
        c.wait()


def place(a_ref, b_ref, c_ref, x_ref, y_ref, z_ref, sem):
    copies = [
        pltpu.make_async_copy(s, d, sem.at[n])
        for n, (s, d) in enumerate(((a_ref, x_ref), (b_ref, y_ref), (c_ref, z_ref)))
    ]
    for c in copies:
        c.start()
    for c in copies:
        c.wait()


def on_device(
    query_rows, key_rows, value_rows, output_grad, output_rows, row_logsumexp,
    chosen_owner, chosen_cubes,
):
    heads = lax.axis_size("head")
    seqs = lax.axis_size("seq")
    piece_rows, full = query_rows.shape[2:]
    width = full // heads
    cubes, sel = chosen_owner.shape
    tokens = row_logsumexp.shape[0]
    rows = tokens // cubes
    piece = piece_rows // rows
    wide = CAP * rows
    half = seqs // 2

    def cubed(a):
        return a.reshape(piece, rows, full)

    bf, f32, i32 = jnp.bfloat16, jnp.float32, jnp.int32
    vmem = pl.BlockSpec(memory_space=pltpu.VMEM)
    anywhere = pl.BlockSpec(memory_space=pl.ANY)
    smem = pl.BlockSpec(memory_space=pltpu.SMEM)
    dma = pltpu.SemaphoreType.DMA
    tok = pltpu.VMEM((cubes, rows, width), bf)
    outs = pl.pallas_call(
        functools.partial(kernel, heads, seqs, sel),
        out_shape=[jax.ShapeDtypeStruct((piece, rows, full), bf)] * 3,
        in_specs=[smem, smem, vmem] + [anywhere] * 5 + [vmem],
        out_specs=[anywhere] * 3,
        scratch_shapes=[
            tok, tok, tok, tok,
            pltpu.VMEM((width, cubes * rows), bf),
            pltpu.VMEM((piece, rows, full), bf),
            pltpu.VMEM((piece, rows, full), bf),
            pltpu.VMEM((heads, piece, 4, wide), f32),
            pltpu.VMEM((cubes, 4, wide), f32),
            pltpu.VMEM((cubes, 4, wide), f32),
            pltpu.SMEM((cubes * sel,), i32),
            pltpu.SMEM((seqs * CAP,), i32),
            pltpu.SMEM((seqs * CAP,), i32),
            pltpu.SMEM((cubes * sel,), i32),
            pltpu.VMEM((sel, cubes), i32),
            pltpu.SMEM((sel, cubes), i32),
            tok, tok,
            pltpu.VMEM((half, 4, wide), f32),
            pltpu.VMEM((half, 4, wide), f32),
            pltpu.SMEM((half * CAP,), i32),
            pltpu.VMEM((half, 2, wide, width), bf),
            pltpu.VMEM((half, 2, wide, width), bf),
            pltpu.VMEM((seqs, 2, wide, width), bf),
            pltpu.VMEM((half, 4, wide), f32),
            pltpu.VMEM((seqs, 4, wide), f32),
            pltpu.VMEM((cubes * rows, width), f32),
            pltpu.VMEM((cubes * rows, width), f32),
            tok, tok, tok,
            pltpu.VMEM((seqs, CAP, rows, width), bf),
            pltpu.VMEM((seqs * CAP, rows, width), bf),
            dma((10,)),
            dma((heads, 5)), dma((heads, 5)),
            dma((2 + 2 * heads,)), dma((2 + 2 * heads,)),
            dma((seqs + half,)), dma((seqs + half,)), dma((seqs,)), dma((seqs,)),
            dma((seqs,)), dma((seqs,)),
            dma((heads, 3)), dma((heads, 3)),
        ],
        compiler_params=pltpu.CompilerParams(collective_id=0, has_side_effects=True),
    )(
        chosen_owner.T, chosen_cubes, chosen_owner.T, cubed(query_rows), cubed(key_rows), cubed(value_rows),
        cubed(output_grad), cubed(output_rows),
        row_logsumexp.reshape(1, tokens),
    )
    outs = pl.pallas_call(
        place,
        out_shape=[jax.ShapeDtypeStruct((piece, rows, full), bf)] * 3,
        in_specs=[anywhere] * 3,
        out_specs=[vmem] * 3,
        scratch_shapes=[dma((3,))],
    )(*outs)
    return tuple(a.reshape(1, 1, piece_rows, full) for a in outs)


def solution(mesh):
    rows = P("seq", "head", None, None)
    return jax.shard_map(
        on_device,
        mesh=mesh,
        in_specs=(rows, rows, rows, rows, rows, P("seq", "head"), P("seq", None), P("seq", None, None)),
        out_specs=(rows, rows, rows),
        check_vma=False,
    )
```
